256 devices in a mesh: wide: 64 (over x, z, core), narrow: 4 (over y).
Axes of the slice: x: 4, y: 4, z: 8, core: 2. Of those that a mesh axis runs over, the one named last changes fastest.
Arguments:
- harvest: bfloat16 [1024, 16384], P('wide', 'narrow'), may hold values from -6 to 6
- pair_ids: int32 [128], P('wide'), may hold values from 0 to 15
- w_enc: bfloat16 [16384, 32768], P('narrow', 'wide'), may hold values from -0.046875 to 0.046875
- b_enc: float32 [32768], P('wide'), may hold values from -3 to 3
- w_dec: bfloat16 [32768, 16384], P('wide', 'narrow'), may hold values from -0.03125 to 0.03125
- b_dec: float32 [16384], P('narrow'), may hold values from -3 to 3
- step_size: float32 [], replicated, may hold values from 0.1 to 0.33
- penalty: float32 [], replicated, may hold values from 0.5 to 2
Outputs:
- latents: float32 [128, 32768], P(None, 'wide')
The draws below stay inside these ranges and needn't reach their ends.
Inputs may be any that keep to these rules, and one draw needn't show every extreme that they name: Token pair b takes pool row (b // 2) * 16 + pair_ids[b].
All inputs are finite; a program needn't handle non-finite values.
Results may differ from the reference program's by a relative error of at most 0.0025.
Values may be sent and summed in bfloat16 or wider, within the bound.
A program may use at most 64 MiB of HBM per device.

```python
import jax
import jax.numpy as jnp
from jax import lax

MODEL_D = 8192
D = 16384
LAT = 32768
ITERS = 2
ROWS_DEV = 2
POOL_DEV = 16
BATCH = 128
POOL = 1024


def with_ends(result, stream_key, low, high):
    longest = result.shape.index(max(result.shape))
    spots = []
    for shift in (0, 1):
        where = [jax.random.randint(jax.random.fold_in(stream_key, axis), (), 0, length) for axis, length in enumerate(result.shape)]
        where[longest] = (where[longest] + shift) % result.shape[longest]
        spots.append(tuple(where))
    return result.at[spots[0]].set(low).at[spots[1]].set(high)


def block_levels(own_key, shape, cuts, smallest, top_value):
    factor_of, own = 1.0, jax.random.fold_in(own_key, 6)
    for axis_at, blocks in cuts:
        steps = jnp.exp(jax.random.uniform(jax.random.fold_in(own, axis_at), (blocks,), jnp.float32, smallest / len(cuts), top_value / len(cuts)))
        factor_of = factor_of * jnp.repeat(steps, shape[axis_at] // blocks).reshape([-1 if axis == axis_at else 1 for axis in range(len(shape))])
    return factor_of


def scatter_about(own_key, dims, spread, most, pieces=(), held_as=jnp.bfloat16):
    drawn = jax.random.normal(own_key, dims, jnp.float32) * spread
    if len(pieces) > 0:
        drawn = block_levels(own_key, dims, pieces, -0.22, 0.18) * drawn
    return jnp.clip(drawn, min=-most, max=most).astype(held_as)


def setup_inputs(seed: int = 0) -> dict:
    key_list = jax.random.split(jax.random.key(seed), 9)
    return {
        "harvest": scatter_about(key_list[0], (POOL, D), 1.0, 6.0, ((0, 64), (1, 4))),
        "pair_ids": with_ends(jax.random.randint(key_list[1], (BATCH,), 0, POOL_DEV), jax.random.fold_in(key_list[1], 1), 0, POOL_DEV - 1).astype(jnp.int32),
        "w_enc": scatter_about(key_list[2], (D, LAT), D ** -0.5, 0.046875, ((0, 4), (1, 64))),
        "b_enc": scatter_about(key_list[3], (LAT,), 0.5, 3.0, ((0, 64),), jnp.float32),
        "w_dec": scatter_about(key_list[4], (LAT, D), LAT ** -0.5, 0.03125, ((0, 64), (1, 4))),
        "b_dec": scatter_about(key_list[5], (D,), 0.5, 3.0, ((0, 4),), jnp.float32),
        "step_size": jnp.clip(jax.random.uniform(key_list[6], (), jnp.float32, 0.1, 0.33), 0.1, 0.33),
        "penalty": jnp.clip(jax.random.uniform(key_list[7], (), jnp.float32, 0.5, 2.0), 0.5, 2.0),
    }


def reference(harvest, pair_ids, w_enc, b_enc, w_dec, b_dec, step_size, penalty):
    index_rows = jnp.arange(BATCH, dtype=jnp.int32) // ROWS_DEV * POOL_DEV + pair_ids.astype(jnp.int32)
    pairs = jnp.take(harvest, index_rows, axis=0)
    pre = jnp.dot(pairs, w_enc, preferred_element_type=jnp.float32)
    decoder = w_dec.astype(jnp.float32)
    norm_base = jnp.sqrt(lax.optimization_barrier(jnp.sum(decoder[:, :MODEL_D] * decoder[:, :MODEL_D], axis=1)))
    norm_inst = jnp.sqrt(lax.optimization_barrier(jnp.sum(decoder[:, MODEL_D:] * decoder[:, MODEL_D:], axis=1)))
    thresh = penalty * step_size * (norm_base + norm_inst)
    latents = jnp.maximum(pre + b_enc, 0.0)
    for step in range(ITERS):
        codes = latents.astype(jnp.bfloat16)
        rebuilt = jnp.dot(codes, w_dec, preferred_element_type=jnp.float32)
        residual = (pairs.astype(jnp.float32) - rebuilt - b_dec).astype(jnp.bfloat16)
        grad = jnp.dot(residual, w_dec.T, preferred_element_type=jnp.float32)
        latents = jnp.maximum(latents + step_size * grad - thresh, 0.0)
    return latents
```

```python
import functools

import jax
import jax.numpy as jnp
from jax import lax
from jax.experimental import pallas as pl
from jax.experimental.pallas import tpu as pltpu
from jax.sharding import PartitionSpec as P

ITERS = 2
X, Z, C, Y = 4, 8, 2, 4
STREAMS = 2
HALF = 2048
FEAT = 256
LAT = 512
LB = 128
ROWS = 64
PR = 16
MESH = pl.DeviceIdType.MESH
F32, BF16 = jnp.float32, jnp.bfloat16
N_SEMS = 200


def nt(a, b):
    return lax.dot_general(a, b, (((1,), (1,)), ((), ())), preferred_element_type=F32)


def nn(a, b):
    return jnp.dot(a, b, preferred_element_type=F32)


def kernel(ids_ref, step_ref, pen_ref, harvest_hbm, wenc_hbm, benc_ref, wdec_hbm, bdec_ref, out_ref,
           harvest_v, wenc_v, wown_v, woth_v, rows_send, rows_recv, piece_v,
           gpair, gpair_oth, sq_acc, sq_send, sq_recv, pre_send, pre_recv,
           codes, pacc, xsend, xrecv, zsend, zrecv, resid, gsend, grecv, ysend, yrecv, fin,
           local_sems, send_sems, recv_sems):
    w, y = lax.axis_index("wide"), lax.axis_index("narrow")
    x, z, c = w // (Z * C), lax.rem(w // C, Z), lax.rem(w, C)

    def dev(x_, z_, c_, y_):
        return ((x_ * Z + z_) * C + c_, y_)

    def at_x(d):
        return dev(lax.rem(x + d, X), z, c, y)

    def at_z(d):
        return dev(x, lax.rem(z + d, Z), c, y)

    def at_y(d):
        return dev(x, z, c, lax.rem(y + d, Y))

    def at_zc(d):
        i = lax.rem(z * C + c + d, Z * C)
        return dev(x, i // C, lax.rem(i, C), y)

    other = dev(x, z, 1 - c, y)

    n_sems = [0]
    sent = []

    def send(src, dst, device):
        i = n_sems[0]
        n_sems[0] += 1
        copy = pltpu.make_async_remote_copy(
            src_ref=src, dst_ref=dst, send_sem=send_sems.at[i], recv_sem=recv_sems.at[i],
            device_id=device, device_id_type=MESH)
        copy.start()
        sent.append(copy)
        return copy

    loads = [
        pltpu.make_async_copy(harvest_hbm, harvest_v, local_sems.at[0]),
        pltpu.make_async_copy(wenc_hbm, wenc_v, local_sems.at[1]),
        pltpu.make_async_copy(wdec_hbm, wown_v, local_sems.at[2]),
    ]
    loads[0].start()

    barrier = pltpu.get_barrier_semaphore()
    partners = [at_zc(d) for d in range(1, Z * C)] + [at_x(d) for d in range(1, X)] + [at_y(d) for d in range(1, Y)]
    for p in partners:
        pl.semaphore_signal(barrier, inc=1, device_id=p, device_id_type=MESH)
    loads[2].start()
    loads[1].start()

    loads[0].wait()
    row = lax.broadcasted_iota(jnp.int32, (PR, PR), 0)
    col = lax.broadcasted_iota(jnp.int32, (PR, PR), 1)
    wanted = jnp.where(row == 0, ids_ref[0], ids_ref[1])
    chooser = jnp.where((row < 2) & (col == wanted), 1.0, 0.0).astype(BF16)
    for i in range(Z * C):
        f0 = (i % C) * HALF + (i // C) * FEAT
        rows_send[i] = nn(chooser, harvest_v[:, f0:f0 + FEAT])[0:2]
    pl.semaphore_wait(barrier, len(partners))

    me = z * C + c
    row_copies = []
    for d in sorted(range(1, Z * C), key=lambda d: -min(d, Z * C - d)):
        i = lax.rem(me + d, Z * C)
        row_copies.append(send(rows_send.at[i], rows_recv.at[me], at_zc(d)))
    h0 = pl.multiple_of(c * HALF, HALF)
    h1 = pl.multiple_of((1 - c) * HALF, HALF)
    w_copy = send(wdec_hbm.at[:, pl.ds(h1, HALF)], woth_v, other)
    rows_recv[me] = rows_send[me]

    def squares():
        loads[2].wait()

        def body(i, carry):
            r0 = pl.multiple_of(i * PR, PR)
            v = wown_v[pl.ds(r0, PR), :].astype(F32)
            v = v * v
            total = v[:, 0:LB]
            for j in range(1, 2 * HALF // LB):
                total = total + v[:, j * LB:(j + 1) * LB]
            sq_acc[pl.ds(r0, PR), :] = total
            return carry

        lax.fori_loop(0, LAT // PR, body, 0)
        ones = jnp.ones((8, LB), BF16)
        rest, flat = sq_acc[...], jnp.zeros((8, LAT), F32)
        for _ in range(3):
            part = rest.astype(BF16)
            flat = flat + nt(ones, part)
            rest = rest - part.astype(F32)
        for j in range(Y):
            sq_send[j] = flat[:, j * LB:(j + 1) * LB]
        copies = []
        for d in (2, 1, 3):
            copies.append(send(sq_send.at[lax.rem(y + d, Y)], sq_recv.at[y], at_y(d)))
        sq_recv[y] = sq_send[y]
        return copies

    sq_copies = []

    def stream(s):
        if s == 0:
            for cp in row_copies:
                cp.wait_recv()
        rid = lax.broadcasted_iota(jnp.int32, (PR, FEAT), 0)
        piece = jnp.zeros((PR, FEAT), F32)
        for i in range(Z):
            for r in range(2):
                line = jnp.broadcast_to(rows_recv[s * Z + i, r:r + 1, :], (PR, FEAT))
                piece = jnp.where(rid == 2 * i + r, line, piece)
        piece_v[s] = piece
        gpair[s, x, z] = piece.astype(BF16)
        cps = [send(gpair.at[s, x, z], gpair.at[s, x, z], at_z(d)) for d in (4, 3, 5, 2, 6, 1, 7)]
        yield
        for cp in cps:
            cp.wait_recv()
        cps = [send(gpair.at[s, x], gpair.at[s, x], at_x(d)) for d in (2, 1, 3)]
        oth = [send(gpair.at[s, x], gpair_oth.at[s, x], other)]
        yield
        if s == 0:
            sq_copies.extend(squares())
            loads[1].wait()
        for d, cp in zip((2, 1, 3), cps):
            cp.wait_recv()
        for d in (2, 1, 3):
            b = lax.rem(x + d, X)
            oth.append(send(gpair.at[s, b], gpair_oth.at[s, b], other))
        acc = jnp.zeros((ROWS, LAT), F32)
        for k in range(Z):
            f0 = pl.multiple_of(c * HALF + k * FEAT, FEAT)
            acc = acc + nn(gpair[s, :, k].reshape(ROWS, FEAT), wenc_v[pl.ds(f0, FEAT), :])
        yield
        for cp in oth:
            cp.wait_recv()
        for k in range(Z):
            f0 = pl.multiple_of((1 - c) * HALF + k * FEAT, FEAT)
            acc = acc + nn(gpair_oth[s, :, k].reshape(ROWS, FEAT), wenc_v[pl.ds(f0, FEAT), :])
        for j in range(Y):
            pre_send[s, j] = acc[:, j * LB:(j + 1) * LB]
        cps = [send(pre_send.at[s, lax.rem(y + d, Y)], pre_recv.at[s, y], at_y(d)) for d in (2, 1, 3)]
        yield
        if s == 0:
            for cp in sq_copies:
                cp.wait_recv()
        for cp in cps:
            cp.wait_recv()
        norm = jnp.sqrt(sq_recv[0] + sq_recv[1]) + jnp.sqrt(sq_recv[2] + sq_recv[3])
        thresh = pen_ref[0] * step_ref[0] * norm[0:1]
        pre_recv[s, y] = pre_send[s, y]
        pre = (pre_recv[s, 0] + pre_recv[s, 1]) + (pre_recv[s, 2] + pre_recv[s, 3])
        latents = jnp.maximum(pre + benc_ref[y], 0.0)
        for t in range(ITERS):
            codes[t, s, c, y] = latents.astype(BF16)
            own = codes.at[t, s, c, y]
            cps = [send(own, own, at_y(d)) for d in (2, 1, 3)]
            oth = [send(own, own, other)]
            yield
            for d, cp in zip((2, 1, 3), cps):
                cp.wait_recv()
            for d in (2, 1, 3):
                o = codes.at[t, s, c, lax.rem(y + d, Y)]
                oth.append(send(o, o, other))
            code = jnp.concatenate([codes[t, s, c, j] for j in range(Y)], axis=1)
            for k in range(X):
                f0 = pl.multiple_of(c * HALF + k * 512, 512)
                pacc[s, :, k * 512:(k + 1) * 512] = nn(code, wown_v[:, pl.ds(f0, 512)])
            yield
            if s == 0 and t == 0:
                w_copy.wait_recv()
            for cp in oth:
                cp.wait_recv()
            code = jnp.concatenate([codes[t, s, 1 - c, j] for j in range(Y)], axis=1)
            for k in range(X):
                part = pacc[s, :, k * 512:(k + 1) * 512] + nn(code, woth_v[:, k * 512:(k + 1) * 512])
                part = part.astype(BF16)
                for j in range(2):
                    xsend[t, s, :, 2 * k + j] = part[:, j * FEAT:(j + 1) * FEAT].reshape(X, PR, FEAT)
            cps = [send(xsend.at[t, s, lax.rem(x + d, X)], xrecv.at[t, s, d - 1], at_x(d)) for d in (2, 1, 3)]
            yield
            for cp in cps:
                cp.wait_recv()
            for k in range(Z):
                total = xsend[t, s, x, k].astype(F32)
                for d in range(X - 1):
                    total = total + xrecv[t, s, d, k].astype(F32)
                zsend[t, s, k] = total.astype(BF16)
            cps = [send(zsend.at[t, s, lax.rem(z + d, Z)], zrecv.at[t, s, d - 1], at_z(d)) for d in (4, 3, 5, 2, 6, 1, 7)]
            yield
            for cp in cps:
                cp.wait_recv()
            total = zsend[t, s, z].astype(F32)
            for d in range(Z - 1):
                total = total + zrecv[t, s, d].astype(F32)
            resid[t, s, x, z] = (piece_v[s] - total - bdec_ref[me]).astype(BF16)
            own = resid.at[t, s, x, z]
            cps = [send(own, own, at_z(d)) for d in (4, 3, 5, 2, 6, 1, 7)]
            yield
            for cp in cps:
                cp.wait_recv()
            own = resid.at[t, s, x]
            cps = [send(own, own, at_x(d)) for d in (2, 1, 3)]
            yield
            for cp in cps:
                cp.wait_recv()
            acc = jnp.zeros((ROWS, LAT), F32)
            for k in range(Z):
                acc = acc + nt(resid[t, s, :, k].reshape(ROWS, FEAT), woth_v[:, k * FEAT:(k + 1) * FEAT])
            gsend[t, s] = acc
            cp_g = send(gsend.at[t, s], grecv.at[t, s], other)
            acc = jnp.zeros((ROWS, LAT), F32)
            for k in range(Z):
                f0 = pl.multiple_of(c * HALF + k * FEAT, FEAT)
                acc = acc + nt(resid[t, s, :, k].reshape(ROWS, FEAT), wown_v[:, pl.ds(f0, FEAT)])
            yield
            cp_g.wait_recv()
            acc = acc + grecv[t, s]
            for j in range(Y):
                ysend[t, s, j] = acc[:, j * LB:(j + 1) * LB].astype(BF16)
            cps = [send(ysend.at[t, s, lax.rem(y + d, Y)], yrecv.at[t, s, y], at_y(d)) for d in (2, 1, 3)]
            yield
            for cp in cps:
                cp.wait_recv()
            yrecv[t, s, y] = ysend[t, s, y]
            grad = yrecv[t, s, 0].astype(F32)
            for j in range(1, Y):
                grad = grad + yrecv[t, s, j].astype(F32)
            latents = jnp.maximum(latents + step_ref[0] * grad - thresh, 0.0)
        own = fin.at[s, y]
        fin[s, y] = latents
        cps = [send(own, own, at_y(d)) for d in (2, 1, 3)]
        yield
        for cp in cps:
            cp.wait_recv()
        for b in range(X):
            r0 = (b * STREAMS + s) * PR
            for j in range(Y):
                out_ref[r0:r0 + PR, j * LB:(j + 1) * LB] = fin[s, j, b * PR:(b + 1) * PR, :]

    running = [stream(s) for s in range(STREAMS)]
    while running:
        for g in list(running):
            try:
                next(g)
            except StopIteration:
                running.remove(g)
    for cp in sent:
        cp.wait_send()


def local(harvest, pair_ids, w_enc, b_enc, w_dec, b_dec, step_size, penalty):
    vm = pltpu.VMEM
    smem = pl.BlockSpec(memory_space=pltpu.SMEM)
    hbm = pl.BlockSpec(memory_space=pl.ANY)
    vmem = pl.BlockSpec(memory_space=pltpu.VMEM)
    S, T = STREAMS, ITERS
    scratch = [
        vm((16, 2 * HALF), BF16), vm((2 * HALF, LAT), BF16), vm((LAT, 2 * HALF), BF16), vm((LAT, HALF), BF16),
        vm((Z * C, 2, FEAT), F32), vm((Z * C, 2, FEAT), F32), vm((S, PR, FEAT), F32),
        vm((S, X, Z, PR, FEAT), BF16), vm((S, X, Z, PR, FEAT), BF16),
        vm((LAT, LB), F32), vm((Y, 8, LB), F32), vm((Y, 8, LB), F32),
        vm((S, Y, ROWS, LB), F32), vm((S, Y, ROWS, LB), F32),
        vm((T, S, C, Y, ROWS, LB), BF16), vm((S, ROWS, HALF), F32),
        vm((T, S, X, Z, PR, FEAT), BF16), vm((T, S, X - 1, Z, PR, FEAT), BF16),
        vm((T, S, Z, PR, FEAT), BF16), vm((T, S, Z - 1, PR, FEAT), BF16),
        vm((T, S, X, Z, PR, FEAT), BF16),
        vm((T, S, ROWS, LAT), F32), vm((T, S, ROWS, LAT), F32),
        vm((T, S, Y, ROWS, LB), BF16), vm((T, S, Y, ROWS, LB), BF16),
        vm((S, Y, ROWS, LB), F32),
        pltpu.SemaphoreType.DMA((3,)), pltpu.SemaphoreType.DMA((N_SEMS,)), pltpu.SemaphoreType.DMA((N_SEMS,)),
    ]
    b_pieces = b_dec.reshape(C, Z, 1, FEAT).transpose(1, 0, 2, 3).reshape(Z * C, 1, FEAT)
    out = pl.pallas_call(
        kernel,
        out_shape=jax.ShapeDtypeStruct((128, LAT), F32),
        in_specs=[smem, smem, smem, hbm, hbm, vmem, hbm, vmem],
        out_specs=vmem,
        scratch_shapes=scratch,
        compiler_params=pltpu.CompilerParams(collective_id=0, has_side_effects=True, vmem_limit_bytes=56 << 20),
        name="ista",
    )(pair_ids, step_size.reshape(1), penalty.reshape(1), harvest, w_enc, b_enc.reshape(Y, 1, LB), w_dec, b_pieces)
    return out


def solution(mesh):
    return jax.shard_map(
        local,
        mesh=mesh,
        in_specs=(
            P("wide", "narrow"),
            P("wide"),
            P("narrow", "wide"),
            P("wide"),
            P("wide", "narrow"),
            P("narrow"),
            P(),
            P(),
        ),
        out_specs=P(None, "wide"),
        check_vma=False,
    )
```

```python
import functools

import jax
import jax.numpy as jnp
from jax import lax
from jax.experimental import pallas as pl
from jax.experimental.pallas import tpu as pltpu
from jax.sharding import PartitionSpec as P

ITERS = 2
X, Z, C, Y = 4, 8, 2, 4
STREAMS = 2
HALF = 2048
FEAT = 256
LAT = 512
LB = 128
ROWS = 64
PR = 16
MESH = pl.DeviceIdType.MESH
F32, BF16 = jnp.float32, jnp.bfloat16
N_SEMS = 260
OFFSET = 4.0
FAR = (4, 3, 5, 2, 6, 1, 7, 0)
NEAR = (0, 1, 7, 2, 6, 3, 5, 4)
PLACE = {d: i for i, d in enumerate(NEAR)}
RUNS = ((0, 1), (1, 3), (3, 5), (5, 7), (7, 8))


def nt(a, b):
    return lax.dot_general(a, b, (((1,), (1,)), ((), ())), preferred_element_type=F32)


def nn(a, b):
    return jnp.dot(a, b, preferred_element_type=F32)


def kernel(ids_ref, step_ref, pen_ref, harvest_hbm, wenc_hbm, benc_ref, wdec_hbm, bdec_ref, out_ref,
           harvest_v, wenc_v, wown_v, woth_v, rows_send, rows_recv,
           wtown_v, wtoth_v, gpair, gpair_oth, sq_acc, sq_all, pre_send, pre_recv, lat, lat_next, acc_v,
           codes, codes_oth, pacc, xsend, xrecv, zsend, zrecv, resid, gsend, grecv, gacc, yall,
           local_sems, send_sems, recv_sems):
    w, y = lax.axis_index("wide"), lax.axis_index("narrow")
    x, z, c = w // (Z * C), lax.rem(w // C, Z), lax.rem(w, C)

    def dev(x_, z_, c_, y_):
        return ((x_ * Z + z_) * C + c_, y_)

    def at_x(d):
        return dev(lax.rem(x + d, X), z, c, y)

    def at_z(d):
        return dev(x, lax.rem(z + d, Z), c, y)

    def at_y(d):
        return dev(x, z, c, lax.rem(y + d, Y))

    def at_zc(d):
        i = lax.rem(z * C + c + d, Z * C)
        return dev(x, i // C, lax.rem(i, C), y)

    other = dev(x, z, 1 - c, y)
    me = z * C + c

    n_sems = [0]
    sent = []

    def send(src, dst, device):
        i = n_sems[0]
        n_sems[0] += 1
        copy = pltpu.make_async_remote_copy(
            src_ref=src, dst_ref=dst, send_sem=send_sems.at[i], recv_sem=recv_sems.at[i],
            device_id=device, device_id_type=MESH)
        copy.start()
        sent.append(copy)
        return copy

    loads = [
        pltpu.make_async_copy(harvest_hbm, harvest_v, local_sems.at[0]),
        pltpu.make_async_copy(wenc_hbm, wenc_v, local_sems.at[1]),
        pltpu.make_async_copy(wdec_hbm, wown_v, local_sems.at[2]),
    ]
    loads[0].start()
    barrier = pltpu.get_barrier_semaphore()
    partners = [at_zc(d) for d in range(1, Z * C)] + [at_x(d) for d in range(1, X)] + [at_y(d) for d in range(1, Y)]
    for p in partners:
        pl.semaphore_signal(barrier, inc=1, device_id=p, device_id_type=MESH)
    loads[2].start()
    loads[1].start()

    loads[0].wait()
    row = lax.broadcasted_iota(jnp.int32, (PR, PR), 0)
    col = lax.broadcasted_iota(jnp.int32, (PR, PR), 1)
    wanted = jnp.where(row == 0, ids_ref[0], ids_ref[1])
    chooser = jnp.where((row < 2) & (col == wanted), 1.0, 0.0).astype(BF16)
    for i in range(C):
        for k in range(4):
            f0 = i * HALF + k * 512
            rows_send[i, :, k * 512:(k + 1) * 512] = nn(chooser, harvest_v[:, f0:f0 + 512])[0:2].astype(BF16)
    pl.semaphore_wait(barrier, len(partners))
    row_copies = []
    for d in sorted(range(1, Z * C), key=lambda d: -min(d, Z * C - d)):
        row_copies.append(send(rows_send.at[lax.rem(c + d, C)], rows_recv.at[me], at_zc(d)))
    h1 = pl.multiple_of((1 - c) * HALF, HALF)
    w_copy = send(wdec_hbm.at[:, pl.ds(h1, HALF)], woth_v, other)
    rows_recv[me] = rows_send[c]

    loads[2].wait()

    def squares(i, carry):
        r0 = pl.multiple_of(i * PR, PR)
        v = wown_v[pl.ds(r0, PR), :].astype(F32)
        v = v * v
        total = v[:, 0:LB]
        for j in range(1, 2 * HALF // LB):
            total = total + v[:, j * LB:(j + 1) * LB]
        sq_acc[pl.ds(r0, PR), :] = total
        return carry

    lax.fori_loop(0, LAT // PR, squares, 0)
    ones = jnp.ones((8, LB), BF16)
    rest, flat = sq_acc[...], jnp.zeros((8, LAT), F32)
    for _ in range(3):
        part = rest.astype(BF16)
        flat = flat + nt(ones, part)
        rest = rest - part.astype(F32)
    sq_all[y] = flat
    sq_copies = [send(sq_all.at[y], sq_all.at[y], at_y(d)) for d in (2, 1, 3)]

    def turned(k, carry):
        f0 = pl.multiple_of(k * FEAT, FEAT)
        wtown_v[pl.ds(f0, FEAT), :] = wown_v[:, pl.ds(pl.multiple_of(c * HALF + k * FEAT, FEAT), FEAT)].T
        return carry

    def turned_oth(k, carry):
        f0 = pl.multiple_of(k * FEAT, FEAT)
        wtoth_v[pl.ds(f0, FEAT), :] = woth_v[:, pl.ds(f0, FEAT)].T
        return carry

    lax.fori_loop(0, Z, turned, 0)

    def stream(s):
        if s == 0:
            for cp in row_copies:
                cp.wait_recv()
        rid = lax.broadcasted_iota(jnp.int32, (8, HALF), 0)
        tops = []
        for top in range(2):
            block = jnp.zeros((8, HALF), F32)
            for i in range(4):
                both = rows_recv[s * Z + top * 4 + i].astype(F32)
                for r in range(2):
                    block = jnp.where(rid == 2 * i + r, jnp.broadcast_to(both[r:r + 1], (8, HALF)), block)
            tops.append(block)
        block = jnp.concatenate(tops, axis=0).astype(BF16)
        for k in range(Z):
            gpair[s, x, k] = block[:, k * FEAT:(k + 1) * FEAT]
        xs, oth = [], []
        for g in (0, 4):
            own = gpair.at[s, x, g:g + 4]
            xs.append([send(own, own, at_x(d)) for d in (2, 1, 3)])
        for g in (0, 4):
            oth.append([send(gpair.at[s, x, g:g + 4], gpair_oth.at[s, x, g:g + 4], other)])
        if s == STREAMS - 1:
            w_copy.wait_recv()
            lax.fori_loop(0, Z, turned_oth, 0)
        yield 0.6, 4.4
        if s == 0:
            loads[1].wait()
        for g in range(2):
            for d, cp in zip((2, 1, 3), xs[g]):
                cp.wait_recv()
                b = lax.rem(x + Y - d, X)
                oth[g].append(send(gpair.at[s, b, 4 * g:4 * g + 4], gpair_oth.at[s, b, 4 * g:4 * g + 4], other))
            for k in range(4 * g, 4 * g + 4):
                f0 = pl.multiple_of(c * HALF + k * FEAT, FEAT)
                part = nn(gpair[s, :, k].reshape(ROWS, FEAT), wenc_v[pl.ds(f0, FEAT), :])
                acc_v[s] = part if k == 0 else acc_v[s] + part
            yield 0.4, 1.4
        for g in range(2):
            for cp in oth[g]:
                cp.wait_recv()
            for k in range(4 * g, 4 * g + 4):
                f0 = pl.multiple_of((1 - c) * HALF + k * FEAT, FEAT)
                acc_v[s] = acc_v[s] + nn(gpair_oth[s, :, k].reshape(ROWS, FEAT), wenc_v[pl.ds(f0, FEAT), :])
        for j in range(Y):
            pre_send[s, j] = acc_v[s, :, j * LB:(j + 1) * LB]
        cps = [send(pre_send.at[s, lax.rem(y + d, Y)], pre_recv.at[s, y], at_y(d)) for d in (2, 1, 3)]
        yield 0.7, 4.5
        for cp in cps:
            cp.wait_recv()
        pre_recv[s, y] = pre_send[s, y]
        pre = (pre_recv[s, 0] + pre_recv[s, 1]) + (pre_recv[s, 2] + pre_recv[s, 3])
        lat[s, y] = jnp.maximum(pre + benc_ref[pl.ds(y, 1), :], 0.0)
        own = lat.at[s, y]
        cps = [send(own, own, at_y(d)) for d in (2, 1, 3)]
        if s == 0:
            for cp in sq_copies:
                cp.wait_recv()
        yield 0.1, 4.5
        for cp in cps:
            cp.wait_recv()
        latents = [lat[s, j] for j in range(Y)]
        for t in range(ITERS):
            code = jnp.concatenate([v.astype(BF16) for v in latents], axis=1)
            codes[t, s] = code
            if t:
                for j in range(Y):
                    lat_next[s, j] = latents[j]
            cp = send(codes.at[t, s], codes_oth.at[t, s], other)
            for i in range(Z):
                k = lax.rem(z + FAR[i], Z)
                f0 = pl.multiple_of(c * HALF + k * FEAT, FEAT)
                pacc[s, i] = nn(code, wown_v[:, pl.ds(f0, FEAT)])
            yield 0.5, 0.6
            cp.wait_recv()
            code = codes_oth[t, s]
            xs = []
            for g in range(4):
                for i in (2 * g, 2 * g + 1):
                    f0 = pl.multiple_of(lax.rem(z + FAR[i], Z) * FEAT, FEAT)
                    part = pacc[s, i] + nn(code, woth_v[:, pl.ds(f0, FEAT)])
                    xsend[t, s, :, i] = part.astype(BF16).reshape(X, PR, FEAT)
                xs.append([send(xsend.at[t, s, lax.rem(x + d, X), 2 * g:2 * g + 2], xrecv.at[t, s, d - 1, 2 * g:2 * g + 2], at_x(d))
                           for d in (2, 1, 3)])
            yield 0.6, 3.2
            zs = []
            for g in range(4):
                for cp in xs[g]:
                    cp.wait_recv()
                for i in (2 * g, 2 * g + 1):
                    total = xsend[t, s, x, i].astype(F32)
                    for d in range(X - 1):
                        total = total + xrecv[t, s, d, i].astype(F32)
                    if FAR[i]:
                        zsend[t, s, i] = total.astype(BF16)
                        zs.append(send(zsend.at[t, s, i], zrecv.at[t, s, i], at_z(FAR[i])))
                if g == 1:
                    yield 0.1, 1.4
            mine = total
            yield 0.1, 3.0
            for i, cp in enumerate(zs):
                cp.wait_recv()
                mine = mine + zrecv[t, s, i].astype(F32)
            b0 = c * (HALF // LB) + z * (FEAT // LB)
            bias = jnp.concatenate([bdec_ref[pl.ds(b0, 1), :], bdec_ref[pl.ds(b0 + 1, 1), :]], axis=1)
            resid[t, s, x, 0] = (gpair[s, x, z].astype(F32) - mine - bias).astype(BF16)
            own = resid.at[t, s, x, 0]
            zs = {d: send(own, resid.at[t, s, x, PLACE[(Z - d) % Z]], at_z(d)) for d in FAR[:-1]}
            xs = []
            for a, b in RUNS:
                if a:
                    for i in range(a, b):
                        zs[(Z - NEAR[i]) % Z].wait_recv()
                run = resid.at[t, s, x, a:b]
                xs.append([send(run, run, at_x(d)) for d in (2, 1, 3)])
                if b in (1, 5):
                    yield 0.2, 2.9
            yield 0.1, 2.6
            for n, (a, b) in enumerate(RUNS):
                for cp in xs[n]:
                    cp.wait_recv()
                for i in range(a, b):
                    k = lax.rem(z + NEAR[i], Z)
                    f0 = pl.multiple_of(k * FEAT, FEAT)
                    part = nn(resid[t, s, :, i].reshape(ROWS, FEAT), wtoth_v[pl.ds(f0, FEAT), :])
                    gsend[t, s] = part if i == 0 else gsend[t, s] + part
                if b == Z:
                    cp = send(gsend.at[t, s], grecv.at[t, s], other)
                for i in range(a, b):
                    k = lax.rem(z + NEAR[i], Z)
                    f0 = pl.multiple_of(k * FEAT, FEAT)
                    part = nn(resid[t, s, :, i].reshape(ROWS, FEAT), wtown_v[pl.ds(f0, FEAT), :])
                    gacc[s] = part if i == 0 else gacc[s] + part
                if b == 5:
                    yield 0.4, 1.6
            yield 0.5, 0.9
            cp.wait_recv()
            yall[t, s, y] = (gacc[s] + grecv[t, s]).astype(BF16)
            own = yall.at[t, s, y]
            cps = [send(own, own, at_y(d)) for d in (2, 1, 3)]
            yield 0.1, 6.0
            for cp in cps:
                cp.wait_recv()
            after = []
            for j in range(Y):
                cols = slice(j * LB, (j + 1) * LB)
                grad = yall[t, s, 0, :, cols].astype(F32)
                for q in range(1, Y):
                    grad = grad + yall[t, s, q, :, cols].astype(F32)
                norm = jnp.sqrt(sq_all[0, 0:1, cols] + sq_all[1, 0:1, cols]) + jnp.sqrt(sq_all[2, 0:1, cols] + sq_all[3, 0:1, cols])
                thresh = pen_ref[0] * step_ref[0] * norm
                after.append((lat_next if t else lat)[s, j] + step_ref[0] * grad - thresh)
            latents = [jnp.maximum(v, 0.0) for v in after]
        for b in range(X):
            r0 = (b * STREAMS + s) * PR
            for j in range(Y):
                out_ref[r0:r0 + PR, j * LB:(j + 1) * LB] = after[j][b * PR:(b + 1) * PR, :]

    now, ready = 0.0, {s: (s * OFFSET, stream(s)) for s in range(STREAMS)}
    while ready:
        s = min(ready, key=lambda k: ready[k][0])
        due, g = ready[s]
        try:
            took, later = next(g)
        except StopIteration:
            del ready[s]
            continue
        now = max(now, due) + took
        ready[s] = (now + later, g)
    for cp in sent:
        cp.wait_send()


def local(harvest, pair_ids, w_enc, b_enc, w_dec, b_dec, step_size, penalty):
    vm = pltpu.VMEM
    smem = pl.BlockSpec(memory_space=pltpu.SMEM)
    hbm = pl.BlockSpec(memory_space=pl.ANY)
    vmem = pl.BlockSpec(memory_space=pltpu.VMEM)
    S, T = STREAMS, ITERS
    scratch = [
        vm((16, 2 * HALF), BF16), vm((2 * HALF, LAT), BF16), vm((LAT, 2 * HALF), BF16), vm((LAT, HALF), BF16),
        vm((C, 2, HALF), BF16), vm((Z * C, 2, HALF), BF16),
        vm((HALF, LAT), BF16), vm((HALF, LAT), BF16),
        vm((S, X, Z, PR, FEAT), BF16), vm((S, X, Z, PR, FEAT), BF16),
        vm((LAT, LB), F32), vm((Y, 8, LAT), F32),
        vm((S, Y, ROWS, LB), F32), vm((S, Y, ROWS, LB), F32), vm((S, Y, ROWS, LB), F32), vm((S, Y, ROWS, LB), F32), vm((S, ROWS, LAT), F32),
        vm((T, S, ROWS, LAT), BF16), vm((T, S, ROWS, LAT), BF16), vm((S, Z, ROWS, FEAT), F32),
        vm((T, S, X, Z, PR, FEAT), BF16), vm((T, S, X - 1, Z, PR, FEAT), BF16),
        vm((T, S, Z, PR, FEAT), BF16), vm((T, S, Z, PR, FEAT), BF16),
        vm((T, S, X, Z, PR, FEAT), BF16),
        vm((T, S, ROWS, LAT), F32), vm((T, S, ROWS, LAT), F32), vm((S, ROWS, LAT), F32),
        vm((T, S, Y, ROWS, LAT), BF16),
        pltpu.SemaphoreType.DMA((3,)), pltpu.SemaphoreType.DMA((N_SEMS,)), pltpu.SemaphoreType.DMA((N_SEMS,)),
    ]
    out = pl.pallas_call(
        kernel,
        out_shape=jax.ShapeDtypeStruct((128, LAT), F32),
        in_specs=[smem, smem, smem, hbm, hbm, vmem, hbm, vmem],
        out_specs=vmem,
        scratch_shapes=scratch,
        compiler_params=pltpu.CompilerParams(collective_id=0, has_side_effects=True, vmem_limit_bytes=56 << 20),
        name="ista",
    )(pair_ids, step_size.reshape(1), penalty.reshape(1), harvest, w_enc, b_enc.reshape(Y, LB), w_dec,
      b_dec.reshape(2 * HALF // LB, LB))
    return jnp.maximum(out, 0.0)


def solution(mesh):
    return jax.shard_map(
        local,
        mesh=mesh,
        in_specs=(
            P("wide", "narrow"),
            P("wide"),
            P("narrow", "wide"),
            P("wide"),
            P("wide", "narrow"),
            P("narrow"),
            P(),
            P(),
        ),
        out_specs=P(None, "wide"),
        check_vma=False,
    )
```

```python
import functools

import jax
import jax.numpy as jnp
from jax import lax
from jax.experimental import pallas as pl
from jax.experimental.pallas import tpu as pltpu
from jax.sharding import PartitionSpec as P

ITERS = 2
X, Z, C, Y = 4, 8, 2, 4
STREAMS = 2
HALF = 2048
FEAT = 256
LAT = 512
LB = 128
ROWS = 64
PR = 16
MESH = pl.DeviceIdType.MESH
F32, BF16 = jnp.float32, jnp.bfloat16
N_SEMS = 260
OFFSET = 4.0
FAR = (4, 3, 5, 2, 6, 1, 7, 0)
NEAR = (0, 1, 7, 2, 6, 3, 5, 4)
PLACE = {d: i for i, d in enumerate(NEAR)}
RUNS = ((0, 1), (1, 3), (3, 5), (5, 7), (7, 8))


def nt(a, b):
    return lax.dot_general(a, b, (((1,), (1,)), ((), ())), preferred_element_type=F32)


def nn(a, b):
    return jnp.dot(a, b, preferred_element_type=F32)


def kernel(ids_ref, step_ref, pen_ref, harvest_hbm, wenc_hbm, benc_ref, wdec_hbm, bdec_ref, out_ref,
           harvest_v, wenc_v, wown_v, woth_v, rows_send, rows_recv,
           wtown_v, wtoth_v, gpair, gpair_oth, sq_acc, sq_all, pre_send, pre_recv, lat, lat_next, acc_v,
           codes, codes_oth, pacc, xsend, xrecv, zsend, zrecv, resid, gsend, grecv, gacc, yall,
           local_sems, send_sems, recv_sems):
    w, y = lax.axis_index("wide"), lax.axis_index("narrow")
    x, z, c = w // (Z * C), lax.rem(w // C, Z), lax.rem(w, C)

    def dev(x_, z_, c_, y_):
        return ((x_ * Z + z_) * C + c_, y_)

    def at_x(d):
        return dev(lax.rem(x + d, X), z, c, y)

    def at_z(d):
        return dev(x, lax.rem(z + d, Z), c, y)

    def at_y(d):
        return dev(x, z, c, lax.rem(y + d, Y))

    def at_zc(d):
        i = lax.rem(z * C + c + d, Z * C)
        return dev(x, i // C, lax.rem(i, C), y)

    other = dev(x, z, 1 - c, y)
    me = z * C + c

    n_sems = [0]
    sent = []

    def send(src, dst, device):
        i = n_sems[0]
        n_sems[0] += 1
        copy = pltpu.make_async_remote_copy(
            src_ref=src, dst_ref=dst, send_sem=send_sems.at[i], recv_sem=recv_sems.at[i],
            device_id=device, device_id_type=MESH)
        copy.start()
        sent.append(copy)
        return copy

    loads = [
        pltpu.make_async_copy(harvest_hbm, harvest_v, local_sems.at[0]),
        pltpu.make_async_copy(wenc_hbm, wenc_v, local_sems.at[1]),
        pltpu.make_async_copy(wdec_hbm, wown_v, local_sems.at[2]),
    ]
    loads[0].start()
    barrier = pltpu.get_barrier_semaphore()
    partners = [at_zc(d) for d in range(1, Z * C)] + [at_x(d) for d in range(1, X)] + [at_y(d) for d in range(1, Y)]
    for p in partners:
        pl.semaphore_signal(barrier, inc=1, device_id=p, device_id_type=MESH)
    loads[2].start()
    loads[1].start()

    loads[0].wait()
    row = lax.broadcasted_iota(jnp.int32, (PR, PR), 0)
    col = lax.broadcasted_iota(jnp.int32, (PR, PR), 1)
    wanted = jnp.where(row == 0, ids_ref[0], ids_ref[1])
    chooser = jnp.where((row < 2) & (col == wanted), 1.0, 0.0).astype(BF16)
    for i in range(C):
        for k in range(4):
            f0 = i * HALF + k * 512
            rows_send[i, :, k * 512:(k + 1) * 512] = nn(chooser, harvest_v[:, f0:f0 + 512])[0:2].astype(BF16)
    pl.semaphore_wait(barrier, len(partners))
    row_copies = []
    for d in sorted(range(1, Z * C), key=lambda d: -min(d, Z * C - d)):
        row_copies.append(send(rows_send.at[lax.rem(c + d, C)], rows_recv.at[me], at_zc(d)))
    h1 = pl.multiple_of((1 - c) * HALF, HALF)
    w_copy = send(wdec_hbm.at[:, pl.ds(h1, HALF)], woth_v, other)
    rows_recv[me] = rows_send[c]

    loads[2].wait()

    def squares(i, carry):
        r0 = pl.multiple_of(i * PR, PR)
        v = wown_v[pl.ds(r0, PR), :].astype(F32)
        v = v * v
        total = v[:, 0:LB]
        for j in range(1, 2 * HALF // LB):
            total = total + v[:, j * LB:(j + 1) * LB]
        sq_acc[pl.ds(r0, PR), :] = total
        return carry

    lax.fori_loop(0, LAT // PR, squares, 0)
    ones = jnp.ones((8, LB), BF16)
    rest, flat = sq_acc[...], jnp.zeros((8, LAT), F32)
    for _ in range(3):
        part = rest.astype(BF16)
        flat = flat + nt(ones, part)
        rest = rest - part.astype(F32)
    sq_all[y] = flat
    sq_copies = [send(sq_all.at[y], sq_all.at[y], at_y(d)) for d in (2, 1, 3)]

    def turned(k, carry):
        f0 = pl.multiple_of(k * FEAT, FEAT)
        wtown_v[pl.ds(f0, FEAT), :] = wown_v[:, pl.ds(pl.multiple_of(c * HALF + k * FEAT, FEAT), FEAT)].T
        return carry

    def turned_oth(k, carry):
        f0 = pl.multiple_of(k * FEAT, FEAT)
        wtoth_v[pl.ds(f0, FEAT), :] = woth_v[:, pl.ds(f0, FEAT)].T
        return carry

    lax.fori_loop(0, Z, turned, 0)

    def stream(s):
        if s == 0:
            for cp in row_copies:
                cp.wait_recv()
        rid = lax.broadcasted_iota(jnp.int32, (8, HALF), 0)
        tops = []
        for top in range(2):
            block = jnp.zeros((8, HALF), F32)
            for i in range(4):
                both = rows_recv[s * Z + top * 4 + i].astype(F32)
                for r in range(2):
                    block = jnp.where(rid == 2 * i + r, jnp.broadcast_to(both[r:r + 1], (8, HALF)), block)
            tops.append(block)
        block = jnp.concatenate(tops, axis=0).astype(BF16)
        for k in range(Z):
            gpair[s, x, k] = block[:, k * FEAT:(k + 1) * FEAT]
        xs, oth = [], []
        for g in (0, 4):
            own = gpair.at[s, x, g:g + 4]
            xs.append([send(own, own, at_x(d)) for d in (2, 1, 3)])
        for g in (0, 4):
            oth.append([send(gpair.at[s, x, g:g + 4], gpair_oth.at[s, x, g:g + 4], other)])
        yield 0.6, 4.4
        if s == 0:
            loads[1].wait()
        for g in range(2):
            for d, cp in zip((2, 1, 3), xs[g]):
                cp.wait_recv()
                b = lax.rem(x + Y - d, X)
                oth[g].append(send(gpair.at[s, b, 4 * g:4 * g + 4], gpair_oth.at[s, b, 4 * g:4 * g + 4], other))
            for k in range(4 * g, 4 * g + 4):
                f0 = pl.multiple_of(c * HALF + k * FEAT, FEAT)
                part = nn(gpair[s, :, k].reshape(ROWS, FEAT), wenc_v[pl.ds(f0, FEAT), :])
                acc_v[s] = part if k == 0 else acc_v[s] + part
            yield 0.4, 1.4
        for g in range(2):
            for cp in oth[g]:
                cp.wait_recv()
            for k in range(4 * g, 4 * g + 4):
                f0 = pl.multiple_of((1 - c) * HALF + k * FEAT, FEAT)
                acc_v[s] = acc_v[s] + nn(gpair_oth[s, :, k].reshape(ROWS, FEAT), wenc_v[pl.ds(f0, FEAT), :])
        for j in range(Y):
            pre_send[s, j] = acc_v[s, :, j * LB:(j + 1) * LB]
        cps = [send(pre_send.at[s, lax.rem(y + d, Y)], pre_recv.at[s, y], at_y(d)) for d in (2, 1, 3)]
        if s == 0:
            w_copy.wait_recv()
            lax.fori_loop(0, Z, turned_oth, 0)
        yield 0.7, 4.5
        for cp in cps:
            cp.wait_recv()
        pre_recv[s, y] = pre_send[s, y]
        pre = (pre_recv[s, 0] + pre_recv[s, 1]) + (pre_recv[s, 2] + pre_recv[s, 3])
        lat[s, y] = jnp.maximum(pre + benc_ref[pl.ds(y, 1), :], 0.0)
        own = lat.at[s, y]
        cps = [send(own, own, at_y(d)) for d in (2, 1, 3)]
        if s == 0:
            for cp in sq_copies:
                cp.wait_recv()
        yield 0.1, 4.5
        for cp in cps:
            cp.wait_recv()
        latents = [lat[s, j] for j in range(Y)]
        for t in range(ITERS):
            code = jnp.concatenate([v.astype(BF16) for v in latents], axis=1)
            codes[t, s] = code
            if t:
                for j in range(Y):
                    lat_next[s, j] = latents[j]
            cp = send(codes.at[t, s], codes_oth.at[t, s], other)
            for i in range(Z):
                k = lax.rem(z + FAR[i], Z)
                f0 = pl.multiple_of(c * HALF + k * FEAT, FEAT)
                pacc[s, i] = nn(code, wown_v[:, pl.ds(f0, FEAT)])
            yield 0.5, 0.6
            cp.wait_recv()
            code = codes_oth[t, s]
            xs = []
            for g in range(4):
                for i in (2 * g, 2 * g + 1):
                    f0 = pl.multiple_of(lax.rem(z + FAR[i], Z) * FEAT, FEAT)
                    part = pacc[s, i] + nn(code, woth_v[:, pl.ds(f0, FEAT)])
                    xsend[t, s, :, i] = part.astype(BF16).reshape(X, PR, FEAT)
                xs.append([send(xsend.at[t, s, lax.rem(x + d, X), 2 * g:2 * g + 2], xrecv.at[t, s, d - 1, 2 * g:2 * g + 2], at_x(d))
                           for d in (2, 1, 3)])
            yield 0.6, 3.2
            zs = []
            for g in range(4):
                for cp in xs[g]:
                    cp.wait_recv()
                for i in (2 * g, 2 * g + 1):
                    total = xsend[t, s, x, i].astype(F32)
                    for d in range(X - 1):
                        total = total + xrecv[t, s, d, i].astype(F32)
                    if FAR[i]:
                        zsend[t, s, i] = total.astype(BF16)
                        zs.append(send(zsend.at[t, s, i], zrecv.at[t, s, i], at_z(FAR[i])))
                if g == 1:
                    yield 0.1, 1.4
            mine = total
            yield 0.1, 3.0
            for i, cp in enumerate(zs):
                cp.wait_recv()
                mine = mine + zrecv[t, s, i].astype(F32)
            b0 = c * (HALF // LB) + z * (FEAT // LB)
            bias = jnp.concatenate([bdec_ref[pl.ds(b0, 1), :], bdec_ref[pl.ds(b0 + 1, 1), :]], axis=1)
            resid[t, s, x, 0] = (gpair[s, x, z].astype(F32) - mine - bias).astype(BF16)
            own = resid.at[t, s, x, 0]
            zs = {d: send(own, resid.at[t, s, x, PLACE[(Z - d) % Z]], at_z(d)) for d in FAR[:-1]}
            xs = []
            for a, b in RUNS:
                if a:
                    for i in range(a, b):
                        zs[(Z - NEAR[i]) % Z].wait_recv()
                run = resid.at[t, s, x, a:b]
                xs.append([send(run, run, at_x(d)) for d in (2, 1, 3)])
                if b in (1, 5):
                    yield 0.2, 2.9
            yield 0.1, 2.6
            for n, (a, b) in enumerate(RUNS):
                for cp in xs[n]:
                    cp.wait_recv()
                for i in range(a, b):
                    k = lax.rem(z + NEAR[i], Z)
                    f0 = pl.multiple_of(k * FEAT, FEAT)
                    part = nn(resid[t, s, :, i].reshape(ROWS, FEAT), wtoth_v[pl.ds(f0, FEAT), :])
                    gsend[t, s] = part if i == 0 else gsend[t, s] + part
                if b == Z:
                    cp = send(gsend.at[t, s], grecv.at[t, s], other)
                for i in range(a, b):
                    k = lax.rem(z + NEAR[i], Z)
                    f0 = pl.multiple_of(k * FEAT, FEAT)
                    part = nn(resid[t, s, :, i].reshape(ROWS, FEAT), wtown_v[pl.ds(f0, FEAT), :])
                    gacc[s] = part if i == 0 else gacc[s] + part
                if b == 5:
                    yield 0.4, 1.6
            yield 0.5, 0.9
            cp.wait_recv()
            yall[t, s, y] = (gacc[s] + grecv[t, s]).astype(BF16)
            own = yall.at[t, s, y]
            cps = [send(own, own, at_y(d)) for d in (2, 1, 3)]
            yield 0.1, 6.0
            for cp in cps:
                cp.wait_recv()
            after = []
            for j in range(Y):
                cols = slice(j * LB, (j + 1) * LB)
                grad = yall[t, s, 0, :, cols].astype(F32)
                for q in range(1, Y):
                    grad = grad + yall[t, s, q, :, cols].astype(F32)
                norm = jnp.sqrt(sq_all[0, 0:1, cols] + sq_all[1, 0:1, cols]) + jnp.sqrt(sq_all[2, 0:1, cols] + sq_all[3, 0:1, cols])
                thresh = pen_ref[0] * step_ref[0] * norm
                after.append((lat_next if t else lat)[s, j] + step_ref[0] * grad - thresh)
            latents = [jnp.maximum(v, 0.0) for v in after]
        for b in range(X):
            r0 = (b * STREAMS + s) * PR
            for j in range(Y):
                out_ref[r0:r0 + PR, j * LB:(j + 1) * LB] = after[j][b * PR:(b + 1) * PR, :]

    now, ready = 0.0, {s: (s * OFFSET, stream(s)) for s in range(STREAMS)}
    while ready:
        s = min(ready, key=lambda k: ready[k][0])
        due, g = ready[s]
        try:
            took, later = next(g)
        except StopIteration:
            del ready[s]
            continue
        now = max(now, due) + took
        ready[s] = (now + later, g)
    for cp in sent:
        cp.wait_send()


def local(harvest, pair_ids, w_enc, b_enc, w_dec, b_dec, step_size, penalty):
    vm = pltpu.VMEM
    smem = pl.BlockSpec(memory_space=pltpu.SMEM)
    hbm = pl.BlockSpec(memory_space=pl.ANY)
    vmem = pl.BlockSpec(memory_space=pltpu.VMEM)
    S, T = STREAMS, ITERS
    scratch = [
        vm((16, 2 * HALF), BF16), vm((2 * HALF, LAT), BF16), vm((LAT, 2 * HALF), BF16), vm((LAT, HALF), BF16),
        vm((C, 2, HALF), BF16), vm((Z * C, 2, HALF), BF16),
        vm((HALF, LAT), BF16), vm((HALF, LAT), BF16),
        vm((S, X, Z, PR, FEAT), BF16), vm((S, X, Z, PR, FEAT), BF16),
        vm((LAT, LB), F32), vm((Y, 8, LAT), F32),
        vm((S, Y, ROWS, LB), F32), vm((S, Y, ROWS, LB), F32), vm((S, Y, ROWS, LB), F32), vm((S, Y, ROWS, LB), F32), vm((S, ROWS, LAT), F32),
        vm((T, S, ROWS, LAT), BF16), vm((T, S, ROWS, LAT), BF16), vm((S, Z, ROWS, FEAT), F32),
        vm((T, S, X, Z, PR, FEAT), BF16), vm((T, S, X - 1, Z, PR, FEAT), BF16),
        vm((T, S, Z, PR, FEAT), BF16), vm((T, S, Z, PR, FEAT), BF16),
        vm((T, S, X, Z, PR, FEAT), BF16),
        vm((T, S, ROWS, LAT), F32), vm((T, S, ROWS, LAT), F32), vm((S, ROWS, LAT), F32),
        vm((T, S, Y, ROWS, LAT), BF16),
        pltpu.SemaphoreType.DMA((3,)), pltpu.SemaphoreType.DMA((N_SEMS,)), pltpu.SemaphoreType.DMA((N_SEMS,)),
    ]
    out = pl.pallas_call(
        kernel,
        out_shape=jax.ShapeDtypeStruct((128, LAT), F32),
        in_specs=[smem, smem, smem, hbm, hbm, vmem, hbm, vmem],
        out_specs=vmem,
        scratch_shapes=scratch,
        compiler_params=pltpu.CompilerParams(collective_id=0, has_side_effects=True, vmem_limit_bytes=56 << 20),
        name="ista",
    )(pair_ids, step_size.reshape(1), penalty.reshape(1), harvest, w_enc, b_enc.reshape(Y, LB), w_dec,
      b_dec.reshape(2 * HALF // LB, LB))
    return jnp.maximum(out, 0.0)


def solution(mesh):
    return jax.shard_map(
        local,
        mesh=mesh,
        in_specs=(
            P("wide", "narrow"),
            P("wide"),
            P("narrow", "wide"),
            P("wide"),
            P("wide", "narrow"),
            P("narrow"),
            P(),
            P(),
        ),
        out_specs=P(None, "wide"),
        check_vma=False,
    )
```
